32 devices in a mesh: dp: 8 (over z, y), tensor: 4 (over x, core).
Axes of the slice: x: 2, y: 2, z: 4, core: 2. Of those that a mesh axis runs over, the one named last changes fastest.
Arguments:
- latents: float32 [32, 4, 32, 32], P('dp'), may hold values from -6 to 6
- noise_draw: float32 [32, 4, 32, 32], P('dp'), may hold values from -6 to 6
- time_index: int32 [32], P('dp'), may hold values from 0 to 999
- plan: float32 [1000], replicated, may hold values from 0.02 to 0.98
- labels: int32 [32], P('dp'), may hold values from 0 to 1000
- loss_weight: float32 [32], P('dp'), may hold values from 0.5 to 2
- features: bfloat16 [8192, 768], P('dp'), may hold values from -6 to 6
- attention_in: float32 [2, 3, 768, 768], P(None, None, 'dp', 'tensor'), may hold values from -0.21875 to 0.21875
- attention_out: float32 [2, 768, 768], P(None, 'tensor', 'dp'), may hold values from -0.875 to 0.875
- feed_expand: float32 [2, 768, 3072], P(None, 'dp', 'tensor'), may hold values from -0.21875 to 0.21875
- feed_reduce: float32 [2, 3072, 768], P(None, 'tensor', 'dp'), may hold values from -0.109375 to 0.109375
- modulation_weight: float32 [768, 10752], P('dp', 'tensor'), may hold values from -0.21875 to 0.21875
- time_first: float32 [256, 768], P('dp'), may hold values from -0.375 to 0.375
- time_second: float32 [768, 768], P('dp'), may hold values from -0.21875 to 0.21875
- class_table: float32 [1001, 768], P(None, 'dp'), may hold values from -6 to 6
- patch_io: float32 [2, 16, 768], P(None, None, 'dp')
- projector_one: float32 [768, 2048], P('dp', 'tensor'), may hold values from -0.21875 to 0.21875
- projector_two: float32 [2048, 2048], P('dp', 'tensor'), may hold values from -0.125 to 0.125
- projector_three: float32 [2048, 768], P('tensor', 'dp'), may hold values from -0.125 to 0.125
Outputs:
- step_attention_in: float32 [2, 3, 768, 768], P(None, None, 'dp', 'tensor')
- step_attention_out: float32 [2, 768, 768], P(None, 'tensor', 'dp')
- step_feed_expand: float32 [2, 768, 3072], P(None, 'dp', 'tensor')
- step_feed_reduce: float32 [2, 3072, 768], P(None, 'tensor', 'dp')
- step_modulation_weight: float32 [768, 10752], P('dp', 'tensor')
- step_time_first: float32 [256, 768], P('dp')
- step_time_second: float32 [768, 768], P('dp')
- step_class_table: float32 [1001, 768], P(None, 'dp')
- step_patch_io: float32 [2, 16, 768], P(None, None, 'dp')
- step_projector_one: float32 [768, 2048], P('dp', 'tensor')
- step_projector_two: float32 [2048, 2048], P('dp', 'tensor')
- step_projector_three: float32 [2048, 768], P('tensor', 'dp')
- new_row_factors: float32 [21513], replicated
- new_column_factors: float32 [33280], replicated
- loss_value: float32 [], replicated
The draws below stay inside these ranges and needn't reach their ends.
All inputs are finite; a program needn't handle non-finite values.
Results may differ from the reference program's by a relative error of at most 0.0208.
The reference program's roundings to bfloat16 on the way count: a program that leaves them out, or rounds other values in their place, can miss the bound.
Values may be sent and summed in bfloat16 or wider, within the bound.
No kernel may reach another device: no remote copies, remote signals or barrier semaphores. Data moves between devices by JAX's collectives and lax.ppermute only.
A program may use at most 192 MiB of HBM per device.

```python
import math
import jax
import jax.numpy as jnp
from jax import lax

D = 768
H = 12
HD = 64
FF = 3072
PH = 2048
ZD = 768
FREQ = 256
CLASSES = 1001
L = 2
CH = 4
SIDE = 32
PSIDE = 2
STEPS = 1000
LATENTS = 32
TPL = 256
PATCH = 16
TOKENS = 8192
MODS = 10752


def draw_patch_io(key, part):
    key_embed = jax.random.fold_in(key, 11)
    key_head = jax.random.fold_in(key, 12)
    embed = jnp.clip(jax.random.normal(key_embed, (PATCH, D), jnp.float32), -6.0, 6.0) * PATCH ** (-0.5)
    head = jnp.clip(jax.random.normal(key_head, (PATCH, D), jnp.float32), -6.0, 6.0) * (256 * D) ** (-0.5)
    return jnp.stack([embed, head]).astype(jnp.float32)


def plant(drawn, own_key, low, largest):
    index_at = [jax.random.randint(jax.random.fold_in(own_key, axis), (), 0, length) for axis, length in enumerate(drawn.shape)]
    main_axis = drawn.shape.index(max(drawn.shape))
    beside = index_at[:main_axis] + [(index_at[main_axis] + 1) % drawn.shape[main_axis]] + index_at[main_axis + 1:]
    return drawn.at[tuple(index_at)].set(low).at[tuple(beside)].set(largest)


def levels(key, shape, shards, low, top_value):
    def one(dim, parts):
        draws = jax.random.uniform(jax.random.fold_in(jax.random.fold_in(key, 6), dim), (parts,), jnp.float32, low / len(shards), top_value / len(shards))
        return jnp.repeat(jnp.exp(draws), shape[dim] // parts).reshape((-1,) + (1,) * (len(shape) - dim - 1))

    factor_of = one(*shards[0])
    for cut in shards[1:]:
        factor_of = factor_of * one(*cut)
    return factor_of


def gaussian(own_key, extent, scale, bound, split=(), kind=jnp.bfloat16):
    loudness = levels(own_key, extent, split, -0.22, 0.18) if split else 1.0
    result = jax.random.normal(own_key, extent, jnp.float32) * scale * loudness
    return jnp.minimum(jnp.maximum(result, -bound), bound).astype(kind)


def setup_inputs(seed: int = 0) -> dict:
    streams_of = jax.random.split(jax.random.key(seed), 20)
    latents = gaussian(streams_of[0], (LATENTS, CH, SIDE, SIDE), 1.0, 6.0, ((0, 8),), jnp.float32)
    noise_draw = gaussian(streams_of[1], (LATENTS, CH, SIDE, SIDE), 1.0, 6.0, ((0, 8),), jnp.float32)
    time_index = plant(jax.random.randint(streams_of[2], (LATENTS,), 0, STEPS), jax.random.fold_in(streams_of[2], 1), 0, STEPS - 1).astype(jnp.int32)
    plan = jnp.clip(jax.random.uniform(streams_of[3], (STEPS,), jnp.float32, 0.02, 0.98), 0.02, 0.98)
    labels = plant(jax.random.randint(streams_of[4], (LATENTS,), 0, CLASSES), jax.random.fold_in(streams_of[4], 1), 0, CLASSES - 1).astype(jnp.int32)
    loss_weight = jnp.clip(0.5 + 1.5 * jax.random.uniform(streams_of[5], (LATENTS,), jnp.float32) ** levels(streams_of[5], (LATENTS,), ((0, 8),), -0.2, 0.2), 0.5, 2.0)
    features = gaussian(streams_of[6], (TOKENS, ZD), 1.0, 6.0, ((0, 8),))
    attention_in = gaussian(streams_of[7], (L, 3, D, D), D ** -0.5, 0.21875, ((2, 8), (3, 4)), jnp.float32)
    attention_out = gaussian(streams_of[8], (L, D, D), (D // 16) ** -0.5, 0.875, ((1, 4), (2, 8)), jnp.float32)
    feed_expand = gaussian(streams_of[9], (L, D, FF), D ** -0.5, 0.21875, ((1, 8), (2, 4)), jnp.float32)
    feed_reduce = gaussian(streams_of[10], (L, FF, D), FF ** -0.5, 0.109375, ((1, 4), (2, 8)), jnp.float32)
    modulation_weight = gaussian(streams_of[11], (D, MODS), D ** -0.5, 0.21875, ((0, 8), (1, 4)), jnp.float32)
    time_first = gaussian(streams_of[12], (FREQ, D), FREQ ** -0.5, 0.375, ((0, 8),), jnp.float32)
    time_second = gaussian(streams_of[13], (D, D), D ** -0.5, 0.21875, ((0, 8),), jnp.float32)
    class_table = gaussian(streams_of[14], (CLASSES, D), 1.0, 6.0, ((1, 8),), jnp.float32)
    patch_io = draw_patch_io(jax.random.fold_in(streams_of[19], 71), 0)
    projector_one = gaussian(streams_of[16], (D, PH), D ** -0.5, 0.21875, ((0, 8), (1, 4)), jnp.float32)
    projector_two = gaussian(streams_of[17], (PH, PH), PH ** -0.5, 0.125, ((0, 8), (1, 4)), jnp.float32)
    projector_three = gaussian(streams_of[18], (PH, ZD), PH ** -0.5, 0.125, ((0, 4), (1, 8)), jnp.float32)
    return {"latents": latents, "noise_draw": noise_draw, "time_index": time_index, "plan": plan, "labels": labels, "loss_weight": loss_weight, "features": features, "attention_in": attention_in, "attention_out": attention_out, "feed_expand": feed_expand, "feed_reduce": feed_reduce, "modulation_weight": modulation_weight, "time_first": time_first, "time_second": time_second, "class_table": class_table, "patch_io": patch_io, "projector_one": projector_one, "projector_two": projector_two, "projector_three": projector_three}


@jax.custom_vjp
def low(v):
    return lax.optimization_barrier(v.astype(jnp.bfloat16)).astype(jnp.float32)

@jax.custom_vjp
def low_back(v):
    return v

def low_keep(v):
    return (low(v), None)

def low_pass(kept, grad):
    return (grad,)

def back_keep(v):
    return (v, None)

def back_low(kept, grad):
    return (low(grad),)
low.defvjp(low_keep, low_pass)
low_back.defvjp(back_keep, back_low)
EPS_NORM = 1e-06
EPS_COS = 1e-06
EPS_FACTOR = 1e-30
LAMBDA_ALIGN = 0.5
RATE = 0.05
CLIP_RMS = 0.5
HIGHEST = lax.Precision.HIGHEST

def product(formula, left_side, right_side):
    return jnp.einsum(formula, left_side, right_side, precision=HIGHEST, preferred_element_type=jnp.float32)

def grid_table(width):
    grid_side = SIDE // PSIDE
    quarter = width // 4
    frequency = 1.0 / 10000.0 ** (jnp.arange(quarter, dtype=jnp.float32) / quarter)
    coords = jnp.arange(grid_side, dtype=jnp.float32)
    angles = coords[:, None] * frequency[None, :]
    single = jnp.concatenate([jnp.sin(angles), jnp.cos(angles)], axis=1)
    across = jnp.broadcast_to(single[None, :, :], (grid_side, grid_side, width // 2))
    downward = jnp.broadcast_to(single[:, None, :], (grid_side, grid_side, width // 2))
    return jnp.concatenate([across, downward], axis=2).reshape(grid_side * grid_side, width)

def time_features(time_values):
    half_width = FREQ // 2
    frequency = jnp.exp(-math.log(10000.0) * jnp.arange(half_width, dtype=jnp.float32) / half_width)
    angles = 1000.0 * time_values[:, None] * frequency[None, :]
    return jnp.concatenate([jnp.cos(angles), jnp.sin(angles)], axis=1)

def patchify(images):
    samples = images.shape[0]
    grid_side = SIDE // PSIDE
    blocks = images.reshape(samples, CH, grid_side, PSIDE, grid_side, PSIDE)
    blocks = jnp.transpose(blocks, (0, 2, 4, 3, 5, 1))
    return blocks.reshape(samples, grid_side * grid_side, PSIDE * PSIDE * CH)

def normalize(values):
    average = lax.optimization_barrier(jnp.mean(values, axis=-1, keepdims=True))
    centred = values - average
    spread = lax.optimization_barrier(jnp.mean(centred * centred, axis=-1, keepdims=True))
    return centred * lax.rsqrt(spread + EPS_NORM)

def attend(modded, joint_weight, output_weight):
    groups = modded.shape[0]
    joined = low_back(low(product('ntd,kde->knte', modded, joint_weight)))
    head_rows = joined.reshape(3, groups, TPL, H, HD)
    scores = low_back(product('nqhe,nkhe->nhqk', head_rows[0], head_rows[1]) * HD ** (-0.5))
    attention = jax.nn.softmax(scores, axis=-1)
    mixed_heads = product('nhqk,nkhe->nqhe', low(attention), head_rows[2]).reshape(groups, TPL, D)
    return low_back(product('nte,ed->ntd', low_back(low(mixed_heads)), output_weight))

def forward(weights, patches, target, time_feat, labels, loss_weight, feature_rows):
    attention_in, attention_out, feed_expand, feed_reduce, modulation_weight, time_first, time_second, class_table, patch_io, projector_one, projector_two, projector_three = [low(weight) for weight in weights]
    samples = patches.shape[0]
    hidden_time = low_back(product('nf,fd->nd', low(time_feat), time_first))
    time_embed = product('nf,fd->nd', low(jax.nn.silu(hidden_time)), time_second)
    condition = low_back(time_embed + class_table[labels])
    modulation = low_back(product('nd,dm->nm', low(jax.nn.silu(condition)), modulation_weight))
    residual = low_back(product('ntp,pd->ntd', low(patches), patch_io[0]) + grid_table(D)[None])
    group_size = math.gcd(samples, 16)
    checked = jax.checkpoint(attend)
    encoded = residual
    for layer_index in range(L):
        pieces = modulation[:, layer_index * 6 * D:(layer_index + 1) * 6 * D].reshape(samples, 6, 1, D)
        modded = low(normalize(residual) * (1.0 + pieces[:, 1]) + pieces[:, 0])
        stacked = modded.reshape(samples // group_size, group_size, TPL, D)
        joint_layer = attention_in[layer_index]
        output_layer = attention_out[layer_index]
        attended = lax.map(lambda block_in: checked(block_in, joint_layer, output_layer), stacked)
        residual = residual + pieces[:, 2] * attended.reshape(samples, TPL, D)
        modded = low(normalize(residual) * (1.0 + pieces[:, 4]) + pieces[:, 3])
        inner_act = low_back(product('ntd,df->ntf', modded, feed_expand[layer_index]))
        branch = low_back(product('ntf,fd->ntd', low(jax.nn.gelu(inner_act, approximate=True)), feed_reduce[layer_index]))
        residual = residual + pieces[:, 5] * branch
        if layer_index == 0:
            encoded = residual
    first_pre = low_back(product('ntd,dh->nth', low(encoded), projector_one))
    second_pre = low_back(product('nth,hg->ntg', low(jax.nn.silu(first_pre)), projector_two))
    latent = low_back(product('ntg,gz->ntz', low(jax.nn.silu(second_pre)), projector_three))
    aligned = lax.optimization_barrier(jnp.sum(latent * feature_rows, axis=-1))
    cosine = aligned * lax.rsqrt(lax.optimization_barrier(jnp.sum(latent * latent, axis=-1)) + EPS_COS) * lax.rsqrt(lax.optimization_barrier(jnp.sum(feature_rows * feature_rows, axis=-1)) + EPS_COS)
    shift_end = modulation[:, L * 6 * D:L * 6 * D + D][:, None, :]
    scale_end = modulation[:, L * 6 * D + D:][:, None, :]
    final_low = low(normalize(residual) * (1.0 + scale_end) + shift_end)
    output = low_back(product('ntd,pd->ntp', final_low, patch_io[1]))
    mismatch = output - target
    velocity = jnp.sum(loss_weight * lax.optimization_barrier(jnp.mean(mismatch * mismatch, axis=(1, 2)))) / LATENTS
    return velocity - LAMBDA_ALIGN * jnp.mean(cosine)

def adafactor(gradient):
    square = gradient * gradient + EPS_FACTOR
    row_new = lax.optimization_barrier(jnp.mean(square, axis=-1))
    column_new = lax.optimization_barrier(jnp.mean(square, axis=-2))
    row_mean = lax.optimization_barrier(jnp.mean(row_new, axis=-1, keepdims=True))
    second = (row_new / row_mean)[..., :, None] * column_new[..., None, :]
    update = gradient * lax.rsqrt(second)
    root_mean = jnp.sqrt(lax.optimization_barrier(jnp.mean(update * update, axis=(-2, -1), keepdims=True)))
    update = update / jnp.maximum(1.0, root_mean / CLIP_RMS)
    return (-RATE * update, row_new, column_new)

def reference(latents, noise_draw, time_index, plan, labels, loss_weight, features, attention_in, attention_out, feed_expand, feed_reduce, modulation_weight, time_first, time_second, class_table, patch_io, projector_one, projector_two, projector_three):
    time_values = plan[time_index]
    time_column = time_values[:, None, None, None]
    noised = (1.0 - time_column) * latents + time_column * noise_draw
    patches = patchify(noised)
    target = patchify(noise_draw - latents)
    time_feat = time_features(time_values)
    feature_rows = features.astype(jnp.float32).reshape(LATENTS, TPL, ZD)
    masters = (attention_in, attention_out, feed_expand, feed_reduce, modulation_weight, time_first, time_second, class_table, patch_io, projector_one, projector_two, projector_three)
    loss_value, pullback = jax.vjp(lambda weights: forward(weights, patches, target, time_feat, labels, loss_weight, feature_rows), masters)
    gradients = pullback(jnp.ones_like(loss_value))[0]
    changes = []
    rows_out = []
    columns_out = []
    for gradient in gradients:
        change, row_new, column_new = adafactor(gradient)
        changes.append(change)
        rows_out.append(row_new.reshape(-1))
        columns_out.append(column_new.reshape(-1))
    return (changes[0], changes[1], changes[2], changes[3], changes[4], changes[5], changes[6], changes[7], changes[8], changes[9], changes[10], changes[11], jnp.concatenate(rows_out), jnp.concatenate(columns_out), loss_value)
```

```python
import functools
import math

import jax
import jax.numpy as jnp
from jax import lax
from jax.experimental import pallas as pl
from jax.experimental.pallas import tpu as pltpu
from jax.sharding import PartitionSpec as P

D = 768
HD = 64
ZD = 768
PH = 2048
FREQ = 256
CLASSES = 1001
L = 2
CH = 4
SIDE = 32
PSIDE = 2
TPL = 256
PATCH = 16
EPS_NORM = 1e-06
EPS_COS = 1e-06
EPS_FACTOR = 1e-30
LAMBDA_ALIGN = 0.5
RATE = 0.05
CLIP_RMS = 0.5
LOW = jnp.bfloat16
FULL = jnp.float32
ANY = pl.BlockSpec(memory_space=pl.ANY)
VM = pl.BlockSpec(memory_space=pltpu.VMEM)
SM = pl.BlockSpec(memory_space=pltpu.SMEM)
QKV = 576
OUTC = 192
FFC = 768
PC = 512


def swap(values, axis, mask):
    size = lax.axis_size(axis)
    return lax.ppermute(values, axis, [(i, i ^ mask) for i in range(size)])


def masks(axis):
    size = lax.axis_size(axis)
    return [1 << b for b in range(size.bit_length() - 1)]


def gather_own_order(values, axis):
    me = lax.axis_index(axis)
    values = values[None]
    for mask in reversed(masks(axis)):
        other = swap(values, axis, mask)
        upper = (me & mask) != 0
        low_part = jnp.where(upper, other, values)
        high_part = jnp.where(upper, values, other)
        values = jnp.stack([low_part, high_part], axis=1)
        values = values.reshape((-1,) + values.shape[2:])
    return values


def gather_relative(values, axis):
    values = values[None]
    for mask in reversed(masks(axis)):
        values = jnp.stack([values, swap(values, axis, mask)], axis=1)
        values = values.reshape((-1,) + values.shape[2:])
    return values


def scatter_own_order(values, axis):
    me = lax.axis_index(axis)
    for mask in masks(axis):
        values = values.reshape((-1, 2) + values.shape[1:])
        upper = (me & mask) != 0
        send = jnp.where(upper, values[:, 0], values[:, 1])
        keep = jnp.where(upper, values[:, 1], values[:, 0])
        values = keep + swap(send, axis, mask)
    return values[0]


def scatter_relative(values, axis):
    for mask in masks(axis):
        values = values.reshape((-1, 2) + values.shape[1:])
        values = values[:, 0] + swap(values[:, 1], axis, mask)
    return values[0]


def total(values, axis):
    for mask in masks(axis):
        values = values + swap(values, axis, mask)
    return values


def orders():
    bits = list(range(len(masks("dp"))))
    high = [b for b in reversed(bits) if b > 0]
    return {
        "A": high + [0, "x"],
        "B": high + ["x", 0],
        "C": [0, "x"] + high,
    }


def gather_weights(shard, order):
    count = len(masks("dp"))
    rows, columns = shard.shape
    values = shard.reshape((1,) * (count + 1) + (rows, columns))
    split = None
    for step in orders()[order]:
        if step == "x":
            other = swap(values, "tensor", 2)
            if order == "A":
                split = (values, other)
            else:
                values = jnp.concatenate([values, other], axis=0)
        else:
            other = swap(values, "dp", 1 << step)
            values = jnp.concatenate([values, other], axis=count - step)
    full = rows * lax.axis_size("dp")
    if split is not None:
        near, far = (v.reshape(full, columns) for v in split)
        arrays = [near, swap(near, "tensor", 1), far, swap(far, "tensor", 1)]
        return arrays, [(0, None), (1, None), (2, None), (3, None)]
    near = values.reshape(2, full, columns)
    arrays = [near, swap(near, "tensor", 1)]
    return arrays, [(0, 0), (1, 0), (0, 1), (1, 1)]


def add(a, b):
    return a.astype(FULL) + b.astype(FULL)


def reduce_gradient(keep, send, order):
    count = len(masks("dp"))
    size = lax.axis_size("dp")
    rows = keep.shape[1] // size
    shape = (2,) * (count + 1) + (rows, keep.shape[2])
    values = add(keep, swap(send, "tensor", 1)).reshape(shape)
    for step in reversed(orders()[order]):
        values = values.astype(LOW)
        axis = 0 if step == "x" else count - step
        near = lax.slice_in_dim(values, 0, 1, axis=axis)
        far = lax.slice_in_dim(values, 1, 2, axis=axis)
        other = swap(far, "tensor", 2) if step == "x" else swap(far, "dp", 1 << step)
        values = add(near, other)
    return values.reshape(rows, keep.shape[2])


def dot(a, b, contract=(1, 0)):
    return lax.dot_general(
        a, b, (((contract[0],), (contract[1],)), ((), ())), preferred_element_type=FULL
    )


def normalize(values):
    average = jnp.mean(values, axis=-1, keepdims=True)
    centred = values - average
    inverse = lax.rsqrt(jnp.mean(centred * centred, axis=-1, keepdims=True) + EPS_NORM)
    return centred * inverse, inverse


def norm_back(grad_norm, normed, inverse):
    return inverse * (
        grad_norm
        - jnp.mean(grad_norm, axis=-1, keepdims=True)
        - normed * jnp.mean(grad_norm * normed, axis=-1, keepdims=True)
    )


def sigmoid(values):
    return 1.0 / (1.0 + jnp.exp(-values))


def silu_slope(values):
    gate = sigmoid(values)
    return gate * (1.0 + values * (1.0 - gate))


GELU_C = math.sqrt(2.0 / math.pi)


def gelu_tanh(values):
    inner = GELU_C * (values + 0.044715 * values * values * values)
    return 0.5 * values * (1.0 + jnp.tanh(inner))


def gelu_slope(values):
    square = values * values
    bent = jnp.tanh(GELU_C * (values + 0.044715 * values * square))
    return 0.5 * (1.0 + bent) + 0.5 * values * (1.0 - bent * bent) * GELU_C * (
        1.0 + 3.0 * 0.044715 * square
    )


def start_loads(refs, places, buffer, sems):
    for s, (which, part) in enumerate(places):
        source = refs[which] if part is None else refs[which].at[part]
        pltpu.make_async_copy(source, buffer.at[s], sems.at[s]).start()


def wait_load(refs, places, buffer, sems, s):
    which, part = places[0]
    source = refs[which] if part is None else refs[which].at[part]
    pltpu.make_async_copy(source, buffer.at[s], sems.at[s]).wait()


def start_store(buffer, keep, send, sems, s):
    for j in range(4):

        @pl.when(s == j)
        def _():
            target = (send if j % 2 else keep).at[j // 2]
            pltpu.make_async_copy(buffer.at[j], target, sems.at[j]).start()


def wait_stores(buffer, keep, send, sems):
    for j in range(4):
        target = (send if j % 2 else keep).at[j // 2]
        pltpu.make_async_copy(buffer.at[j], target, sems.at[j]).wait()


def params():
    return pltpu.CompilerParams(vmem_limit_bytes=60 * 1024 * 1024)


def cost(flops, size):
    return pl.CostEstimate(flops=flops, bytes_accessed=size, transcendentals=0)


def attn_heads(joined, h):
    return (
        joined[:, h * HD : (h + 1) * HD],
        joined[:, OUTC + h * HD : OUTC + (h + 1) * HD],
        joined[:, 2 * OUTC + h * HD : 2 * OUTC + (h + 1) * HD],
    )


def softmax_rows(query, key):
    scores = dot(query, key, (1, 1)) * HD ** (-0.5)
    exponent = jnp.exp(scores - jnp.max(scores, axis=-1, keepdims=True))
    return exponent / jnp.sum(exponent, axis=-1, keepdims=True)


def attn_forward_kernel(row, count, places, x_ref, m_ref, *refs):
    w_refs = refs[:count]
    out_ref, joined_ref, mixed_ref, attended_ref, wbuf, modded, sems = refs[count:]
    start_loads(w_refs, places, wbuf, sems)
    normed, _ = normalize(x_ref[...])
    modded[...] = (normed * (1.0 + m_ref[row + 1 : row + 2]) + m_ref[row : row + 1]).astype(LOW)
    attended_ref[...] = jnp.zeros_like(attended_ref)

    def block(s, carry):
        wait_load(w_refs, places, wbuf, sems, s)
        joined_ref[s] = dot(modded[...], wbuf[s, :, :QKV]).astype(LOW)
        joined = joined_ref[s]
        parts = []
        for h in range(OUTC // HD):
            query, key, value = attn_heads(joined, h)
            parts.append(dot(softmax_rows(query, key).astype(LOW), value).astype(LOW))
        mixed_ref[s] = jnp.concatenate(parts, axis=1)
        attended_ref[...] += dot(mixed_ref[s], wbuf[s, :, QKV:], (1, 1))
        return carry

    lax.fori_loop(0, 4, block, 0)
    out_ref[...] = x_ref[...] + m_ref[row + 2 : row + 3] * attended_ref[...]


def attn_forward(x, mods, row, weights):
    arrays, places = weights
    count = len(arrays)
    return pl.pallas_call(
        functools.partial(attn_forward_kernel, row, count, places),
        in_specs=[VM, VM] + [ANY] * count,
        out_specs=[VM] * 4,
        out_shape=[
            jax.ShapeDtypeStruct((TPL, D), FULL),
            jax.ShapeDtypeStruct((4, TPL, QKV), LOW),
            jax.ShapeDtypeStruct((4, TPL, OUTC), LOW),
            jax.ShapeDtypeStruct((TPL, D), FULL),
        ],
        scratch_shapes=[
            pltpu.VMEM((4, D, D), LOW),
            pltpu.VMEM((TPL, D), LOW),
            pltpu.SemaphoreType.DMA((4,)),
        ],
        compiler_params=params(),
        cost_estimate=cost(2 * TPL * D * D * 4 + 12 * TPL * TPL * HD * 4, 8 * 1024 * 1024),
        name="attn_fwd",
    )(x, mods, *arrays)


def ffn_forward_kernel(row, count, places, x_ref, m_ref, *refs):
    w_refs = refs[:count]
    out_ref, inner_ref, branch_ref, wbuf, modded, sems = refs[count:]
    start_loads(w_refs, places, wbuf, sems)
    normed, _ = normalize(x_ref[...])
    modded[...] = (normed * (1.0 + m_ref[row + 1 : row + 2]) + m_ref[row : row + 1]).astype(LOW)
    branch_ref[...] = jnp.zeros_like(branch_ref)

    def block(s, carry):
        wait_load(w_refs, places, wbuf, sems, s)
        inner_ref[s] = dot(modded[...], wbuf[s, :, :FFC])
        activated = gelu_tanh(inner_ref[s]).astype(LOW)
        branch_ref[...] += dot(activated, wbuf[s, :, FFC:], (1, 1))
        return carry

    lax.fori_loop(0, 4, block, 0)
    out_ref[...] = x_ref[...] + m_ref[row + 2 : row + 3] * branch_ref[...]


def ffn_forward(x, mods, row, weights):
    arrays, places = weights
    count = len(arrays)
    return pl.pallas_call(
        functools.partial(ffn_forward_kernel, row, count, places),
        in_specs=[VM, VM] + [ANY] * count,
        out_specs=[VM] * 3,
        out_shape=[
            jax.ShapeDtypeStruct((TPL, D), FULL),
            jax.ShapeDtypeStruct((4, TPL, FFC), FULL),
            jax.ShapeDtypeStruct((TPL, D), FULL),
        ],
        scratch_shapes=[
            pltpu.VMEM((4, D, 2 * FFC), LOW),
            pltpu.VMEM((TPL, D), LOW),
            pltpu.SemaphoreType.DMA((4,)),
        ],
        compiler_params=params(),
        cost_estimate=cost(4 * TPL * D * FFC * 4, 16 * 1024 * 1024),
        name="ffn_fwd",
    )(x, mods, *arrays)


def finish_norm(dx, dmod, normed, inverse, scale, dx_ref, dm_ref, row, gate_grad):
    dm_ref[...] = jnp.zeros_like(dm_ref)
    dm_ref[0:1] = jnp.sum(dmod, axis=0, keepdims=True)
    dm_ref[1:2] = jnp.sum(dmod * normed, axis=0, keepdims=True)
    dm_ref[2:3] = gate_grad
    dx_ref[...] = dx + norm_back(dmod * (1.0 + scale), normed, inverse)


def ffn_backward_kernel(row, count, places, up_ref, x_ref, m_ref, inner_ref, branch_ref, *refs):
    w_refs = refs[:count]
    (dx_ref, dm_ref, keep, send, wbuf, dbuf, modded, grad, dmod, sems, osems) = refs[count:]
    start_loads(w_refs, places, wbuf, sems)
    scale = m_ref[row + 1 : row + 2]
    normed, inverse = normalize(x_ref[...])
    modded[...] = (normed * (1.0 + scale) + m_ref[row : row + 1]).astype(LOW)
    grad[...] = (up_ref[...] * m_ref[row + 2 : row + 3]).astype(LOW)
    dmod[...] = jnp.zeros_like(dmod)

    def block(s, carry):
        wait_load(w_refs, places, wbuf, sems, s)
        activated = gelu_tanh(inner_ref[s]).astype(LOW)
        dbuf[s, :, FFC:] = dot(grad[...], activated, (0, 0)).astype(LOW)
        grad_act = dot(grad[...], wbuf[s, :, FFC:])
        grad_inner = (grad_act * gelu_slope(inner_ref[s])).astype(LOW)
        dbuf[s, :, :FFC] = dot(modded[...], grad_inner, (0, 0)).astype(LOW)
        dmod[...] += dot(grad_inner, wbuf[s, :, :FFC], (1, 1))
        start_store(dbuf, keep, send, osems, s)
        return carry

    lax.fori_loop(0, 4, block, 0)
    gate_grad = jnp.sum(up_ref[...] * branch_ref[...], axis=0, keepdims=True)
    normed, inverse = normalize(x_ref[...])
    finish_norm(up_ref[...], dmod[...], normed, inverse, scale, dx_ref, dm_ref, row, gate_grad)
    wait_stores(dbuf, keep, send, osems)


def ffn_backward(upstream, x, mods, row, inner, branch, weights):
    arrays, places = weights
    count = len(arrays)
    return pl.pallas_call(
        functools.partial(ffn_backward_kernel, row, count, places),
        in_specs=[VM] * 5 + [ANY] * count,
        out_specs=[VM, VM, ANY, ANY],
        out_shape=[
            jax.ShapeDtypeStruct((TPL, D), FULL),
            jax.ShapeDtypeStruct((8, D), FULL),
            jax.ShapeDtypeStruct((2, D, 2 * FFC), LOW),
            jax.ShapeDtypeStruct((2, D, 2 * FFC), LOW),
        ],
        scratch_shapes=[
            pltpu.VMEM((4, D, 2 * FFC), LOW),
            pltpu.VMEM((4, D, 2 * FFC), LOW),
            pltpu.VMEM((TPL, D), LOW),
            pltpu.VMEM((TPL, D), LOW),
            pltpu.VMEM((TPL, D), FULL),
            pltpu.SemaphoreType.DMA((4,)),
            pltpu.SemaphoreType.DMA((4,)),
        ],
        compiler_params=params(),
        cost_estimate=cost(8 * TPL * D * FFC * 4, 28 * 1024 * 1024),
        name="ffn_bwd",
    )(upstream, x, mods, inner, branch, *arrays)


def attn_backward_kernel(
    row, count, places, up_ref, x_ref, m_ref, joined_ref, mixed_ref, attended_ref, *refs
):
    w_refs = refs[:count]
    (dx_ref, dm_ref, keep, send, wbuf, dbuf, modded, grad, dmod, joined_grad, sems, osems) = refs[
        count:
    ]
    start_loads(w_refs, places, wbuf, sems)
    scale = m_ref[row + 1 : row + 2]
    normed, inverse = normalize(x_ref[...])
    modded[...] = (normed * (1.0 + scale) + m_ref[row : row + 1]).astype(LOW)
    grad[...] = (up_ref[...] * m_ref[row + 2 : row + 3]).astype(LOW)
    dmod[...] = jnp.zeros_like(dmod)
    factor = HD ** (-0.5)

    def block(s, carry):
        wait_load(w_refs, places, wbuf, sems, s)
        dbuf[s, :, QKV:] = dot(grad[...], mixed_ref[s], (0, 0)).astype(LOW)
        grad_mixed = dot(grad[...], wbuf[s, :, QKV:]).astype(LOW)
        joined = joined_ref[s]
        queries, keys, values = [], [], []
        for h in range(OUTC // HD):
            query, key, value = attn_heads(joined, h)
            own = grad_mixed[:, h * HD : (h + 1) * HD]
            attention = softmax_rows(query, key)
            values.append(dot(attention.astype(LOW), own, (0, 0)).astype(LOW))
            grad_attention = dot(own, value, (1, 1))
            grad_scores = attention * (
                grad_attention - jnp.sum(attention * grad_attention, axis=-1, keepdims=True)
            )
            grad_scores = grad_scores.astype(LOW)
            queries.append((dot(grad_scores, key) * factor).astype(LOW))
            keys.append((dot(grad_scores, query, (0, 0)) * factor).astype(LOW))
        joined_grad[...] = jnp.concatenate(queries + keys + values, axis=1)
        dbuf[s, :, :QKV] = dot(modded[...], joined_grad[...], (0, 0)).astype(LOW)
        dmod[...] += dot(joined_grad[...], wbuf[s, :, :QKV], (1, 1))
        start_store(dbuf, keep, send, osems, s)
        return carry

    lax.fori_loop(0, 4, block, 0)
    gate_grad = jnp.sum(up_ref[...] * attended_ref[...], axis=0, keepdims=True)
    normed, inverse = normalize(x_ref[...])
    finish_norm(up_ref[...], dmod[...], normed, inverse, scale, dx_ref, dm_ref, row, gate_grad)
    wait_stores(dbuf, keep, send, osems)


def attn_backward(upstream, x, mods, row, joined, mixed, attended, weights):
    arrays, places = weights
    count = len(arrays)
    return pl.pallas_call(
        functools.partial(attn_backward_kernel, row, count, places),
        in_specs=[VM] * 6 + [ANY] * count,
        out_specs=[VM, VM, ANY, ANY],
        out_shape=[
            jax.ShapeDtypeStruct((TPL, D), FULL),
            jax.ShapeDtypeStruct((8, D), FULL),
            jax.ShapeDtypeStruct((2, D, D), LOW),
            jax.ShapeDtypeStruct((2, D, D), LOW),
        ],
        scratch_shapes=[
            pltpu.VMEM((4, D, D), LOW),
            pltpu.VMEM((4, D, D), LOW),
            pltpu.VMEM((TPL, D), LOW),
            pltpu.VMEM((TPL, D), LOW),
            pltpu.VMEM((TPL, D), FULL),
            pltpu.VMEM((TPL, QKV), LOW),
            pltpu.SemaphoreType.DMA((4,)),
            pltpu.SemaphoreType.DMA((4,)),
        ],
        compiler_params=params(),
        cost_estimate=cost(4 * TPL * D * D * 4 + 12 * TPL * TPL * HD * 12, 16 * 1024 * 1024),
        name="attn_bwd",
    )(upstream, x, mods, joined, mixed, attended, *arrays)


def projector_kernel(
    blocks, scale, counts, places_a, places_b, key_ref, x_ref, feature_ref, *refs
):
    count_a, count_b = counts
    a_refs = refs[:count_a]
    b_refs = refs[count_a : count_a + count_b]
    (
        dx_ref,
        cos_ref,
        keep_a,
        send_a,
        keep_b,
        send_b,
        wa,
        wb,
        da,
        db,
        encoded,
        first_pre,
        first_all,
        second_pre,
        second_low,
        back_all,
        latent,
        grad_latent,
        sems_a,
        sems_b,
        osems_a,
        osems_b,
    ) = refs[count_a + count_b :]
    width = PH // blocks
    per = PC // width
    start_loads(a_refs, places_a, wa, sems_a)
    start_loads(b_refs, places_b, wb, sems_b)
    key = key_ref[0]
    encoded[...] = x_ref[...].astype(LOW)
    latent[...] = jnp.zeros_like(latent)
    back_all[...] = jnp.zeros_like(back_all)

    def rows(r):
        return pl.ds(pl.multiple_of(r * width, width), width)

    def first(s, carry):
        wait_load(a_refs, places_a, wa, sems_a, s)
        first_pre[s] = dot(encoded[...], wa[s, :, :PC])
        value = first_pre[s]
        value = (value * sigmoid(value)).astype(LOW)
        for h in range(per):
            first_all[lax.bitwise_xor(key, s * per + h)] = value[:, h * width : (h + 1) * width]
        return carry

    lax.fori_loop(0, 4, first, 0)

    def second(s, carry):
        wait_load(b_refs, places_b, wb, sems_b, s)

        def inner(r, total_pre):
            return total_pre + dot(first_all[r], wb[s, rows(r), :])

        value = lax.fori_loop(0, blocks, inner, jnp.zeros((TPL, PC), FULL))
        second_pre[s] = value
        second_low[s] = (value * sigmoid(value)).astype(LOW)
        latent[...] += dot(second_low[s], wa[s, :, PC:], (1, 1))
        return carry

    lax.fori_loop(0, 4, second, 0)
    feature_rows = feature_ref[...].astype(FULL)
    latent_rows = latent[...]
    aligned = jnp.sum(latent_rows * feature_rows, axis=-1, keepdims=True)
    inv_latent = lax.rsqrt(jnp.sum(latent_rows * latent_rows, axis=-1, keepdims=True) + EPS_COS)
    inv_feature = lax.rsqrt(jnp.sum(feature_rows * feature_rows, axis=-1, keepdims=True) + EPS_COS)
    cosine = aligned * inv_latent * inv_feature
    cos_ref[...] = jnp.broadcast_to(jnp.sum(cosine, axis=0, keepdims=True), cos_ref.shape)
    grad_latent[...] = (
        scale
        * inv_feature
        * (
            feature_rows * inv_latent
            - aligned * (inv_latent * inv_latent * inv_latent) * latent_rows
        )
    ).astype(LOW)

    def third(s, carry):
        da[s, :, PC:] = dot(grad_latent[...], second_low[s], (0, 0)).astype(LOW)
        upstream = dot(grad_latent[...], wa[s, :, PC:])
        second_low[s] = (upstream * silu_slope(second_pre[s])).astype(LOW)

        def inner(r, unused):
            db[s, rows(r), :] = dot(first_all[r], second_low[s], (0, 0)).astype(LOW)
            back_all[r] += dot(second_low[s], wb[s, rows(r), :], (1, 1))
            return unused

        lax.fori_loop(0, blocks, inner, 0)
        start_store(db, keep_b, send_b, osems_b, s)
        return carry

    lax.fori_loop(0, 4, third, 0)
    dx_ref[...] = jnp.zeros_like(dx_ref)

    def fourth(s, carry):
        upstream = jnp.concatenate(
            [back_all[lax.bitwise_xor(key, s * per + h)] for h in range(per)], axis=1
        )
        grad_first = (upstream * silu_slope(first_pre[s])).astype(LOW)
        da[s, :, :PC] = dot(encoded[...], grad_first, (0, 0)).astype(LOW)
        dx_ref[...] += dot(grad_first, wa[s, :, :PC], (1, 1))
        start_store(da, keep_a, send_a, osems_a, s)
        return carry

    lax.fori_loop(0, 4, fourth, 0)
    wait_stores(db, keep_b, send_b, osems_b)
    wait_stores(da, keep_a, send_a, osems_a)


def projector(x, features, key, scale, weights_a, weights_b):
    arrays_a, places_a = weights_a
    arrays_b, places_b = weights_b
    counts = (len(arrays_a), len(arrays_b))
    blocks = lax.axis_size("dp")
    width = PH // blocks
    return pl.pallas_call(
        functools.partial(projector_kernel, blocks, scale, counts, places_a, places_b),
        in_specs=[SM, VM, VM] + [ANY] * sum(counts),
        out_specs=[VM, VM] + [ANY] * 4,
        out_shape=[
            jax.ShapeDtypeStruct((TPL, D), FULL),
            jax.ShapeDtypeStruct((8, 128), FULL),
            jax.ShapeDtypeStruct((2, D, 2 * PC), LOW),
            jax.ShapeDtypeStruct((2, D, 2 * PC), LOW),
            jax.ShapeDtypeStruct((2, PH, PC), LOW),
            jax.ShapeDtypeStruct((2, PH, PC), LOW),
        ],
        scratch_shapes=[
            pltpu.VMEM((4, D, 2 * PC), LOW),
            pltpu.VMEM((4, PH, PC), LOW),
            pltpu.VMEM((4, D, 2 * PC), LOW),
            pltpu.VMEM((4, PH, PC), LOW),
            pltpu.VMEM((TPL, D), LOW),
            pltpu.VMEM((4, TPL, PC), FULL),
            pltpu.VMEM((blocks, TPL, width), LOW),
            pltpu.VMEM((4, TPL, PC), FULL),
            pltpu.VMEM((4, TPL, PC), LOW),
            pltpu.VMEM((blocks, TPL, width), FULL),
            pltpu.VMEM((TPL, ZD), FULL),
            pltpu.VMEM((TPL, ZD), LOW),
            pltpu.SemaphoreType.DMA((4,)),
            pltpu.SemaphoreType.DMA((4,)),
            pltpu.SemaphoreType.DMA((4,)),
            pltpu.SemaphoreType.DMA((4,)),
        ],
        compiler_params=params(),
        cost_estimate=cost(6 * TPL * (D * PH + PH * PH + PH * ZD), 32 * 1024 * 1024),
        name="projector",
    )(key, x, features, *arrays_a, *arrays_b)


def head_kernel(row, scale, x_ref, m_ref, w_ref, target_ref, weight_ref, *outs):
    dx_ref, dm_ref, dw_ref, loss_ref = outs
    scale_end = m_ref[row + 1 : row + 2]
    normed, inverse = normalize(x_ref[...])
    final_low = (normed * (1.0 + scale_end) + m_ref[row : row + 1]).astype(LOW)
    output = dot(final_low, w_ref[...], (1, 1))
    mismatch = output - target_ref[...]
    squares = jnp.sum(jnp.sum(mismatch * mismatch, axis=1, keepdims=True), axis=0, keepdims=True)
    loss_ref[...] = jnp.broadcast_to(squares, loss_ref.shape)
    grad_out = (weight_ref[0] * scale * mismatch).astype(LOW)
    dw_ref[...] = dot(grad_out, final_low, (0, 0))
    dmod = dot(grad_out, w_ref[...])
    dm_ref[...] = jnp.zeros_like(dm_ref)
    dm_ref[0:1] = jnp.sum(dmod, axis=0, keepdims=True)
    dm_ref[1:2] = jnp.sum(dmod * normed, axis=0, keepdims=True)
    dx_ref[...] = norm_back(dmod * (1.0 + scale_end), normed, inverse)


def head(x, mods, row, weights, target, weight, scale):
    return pl.pallas_call(
        functools.partial(head_kernel, row, scale),
        in_specs=[VM] * 4 + [SM],
        out_specs=[VM] * 4,
        out_shape=[
            jax.ShapeDtypeStruct((TPL, D), FULL),
            jax.ShapeDtypeStruct((8, D), FULL),
            jax.ShapeDtypeStruct((PATCH, D), FULL),
            jax.ShapeDtypeStruct((8, 128), FULL),
        ],
        compiler_params=params(),
        cost_estimate=cost(6 * TPL * D * PATCH, 2 * 1024 * 1024),
        name="head",
    )(x, mods, weights, target, weight)


def matmul(formula, left_side, right_side):
    return jnp.einsum(formula, left_side, right_side, preferred_element_type=FULL)


def time_features(time_values):
    half_width = FREQ // 2
    frequency = jnp.exp(-math.log(10000.0) * jnp.arange(half_width, dtype=FULL) / half_width)
    angles = 1000.0 * time_values[:, None] * frequency[None, :]
    return jnp.concatenate([jnp.cos(angles), jnp.sin(angles)], axis=1)


def patchify(image):
    grid_side = SIDE // PSIDE
    blocks = image.reshape(CH, grid_side, PSIDE, grid_side, PSIDE)
    blocks = jnp.transpose(blocks, (1, 3, 2, 4, 0))
    return blocks.reshape(grid_side * grid_side, PSIDE * PSIDE * CH)


def relative_columns(width, size, me):
    part = width // size
    column = lax.iota(jnp.int32, width)
    return ((column // part) ^ me) * part + column % part


def grid_table(absolute):
    grid_side = SIDE // PSIDE
    half = D // 2
    quarter = D // 4
    within = absolute % half
    exponent = (within % quarter).astype(FULL) / quarter
    frequency = 1.0 / 10000.0**exponent
    coords = jnp.arange(grid_side, dtype=FULL)
    angles = coords[:, None] * frequency[None, :]
    single = jnp.where(within[None, :] < quarter, jnp.sin(angles), jnp.cos(angles))
    shape = (grid_side, grid_side, D)
    across = jnp.broadcast_to(single[None, :, :], shape)
    downward = jnp.broadcast_to(single[:, None, :], shape)
    return jnp.where(absolute < half, across, downward).reshape(grid_side * grid_side, D)


def flip_blocks(values, size, me):
    shape = values.shape
    bits = size.bit_length() - 1
    values = values.reshape(shape[:-1] + (2,) * bits + (shape[-1] // size,))
    lead = len(shape) - 1
    for b in range(bits):
        axis = lead + bits - 1 - b
        values = jnp.where((me >> b) & 1 == 1, jnp.flip(values, axis), values)
    return values.reshape(shape)


def own_sample(values, index):
    return lax.dynamic_index_in_dim(values, index, 0, keepdims=False)


def body(
    latents,
    noise_draw,
    time_index,
    plan,
    labels,
    loss_weight,
    features,
    attention_in,
    attention_out,
    feed_expand,
    feed_reduce,
    modulation_weight,
    time_first,
    time_second,
    class_table,
    patch_io,
    projector_one,
    projector_two,
    projector_three,
):
    size = lax.axis_size("dp")
    dp_rank = lax.axis_index("dp")
    tensor_rank = lax.axis_index("tensor")
    samples = latents.shape[0]
    latent_count = samples * size
    part = D // size

    step_iota = lax.broadcasted_iota(jnp.int32, (samples, plan.shape[0]), 1)
    time_values = jnp.sum(jnp.where(time_index[:, None] == step_iota, plan[None, :], 0.0), axis=1)
    facts = gather_own_order(jnp.stack([time_values, labels.astype(FULL)]), "dp")
    all_times = facts[:, 0].reshape(-1)
    all_labels = facts[:, 1].reshape(-1).astype(jnp.int32)
    time_rows = jnp.concatenate([time_first.astype(LOW), time_second.astype(LOW)], axis=0)
    quarter = D // 4
    time_rows = lax.dynamic_slice_in_dim(time_rows, tensor_rank * quarter, quarter, 1)
    time_rows = gather_own_order(gather_own_order(time_rows, "dp"), "tensor")
    time_rows = jnp.transpose(time_rows, (1, 2, 0, 3)).reshape(size, -1, D)
    time_one = time_rows[:, : FREQ // size].reshape(FREQ, D)
    time_two = time_rows[:, FREQ // size :].reshape(D, D)

    def transposed(values):
        return jnp.swapaxes(values, -1, -2)

    gathered = {}
    for layer in range(L):
        joint = jnp.moveaxis(attention_in[layer], 0, 1).reshape(part, QKV)
        shard = jnp.concatenate([joint, transposed(attention_out[layer])], axis=1).astype(LOW)
        gathered["a", layer] = gather_weights(shard, "A")
        shard = jnp.concatenate([feed_expand[layer], transposed(feed_reduce[layer])], axis=1)
        gathered["f", layer] = gather_weights(shard.astype(LOW), "BC"[layer])
    shard = jnp.concatenate([projector_one, transposed(projector_three)], axis=1).astype(LOW)
    gathered["p"] = gather_weights(shard, "B")
    gathered["q"] = gather_weights(projector_two.astype(LOW), "A")
    edge = gather_relative(patch_io.astype(LOW), "dp")
    edge = jnp.moveaxis(edge, 0, 2).reshape(2, PATCH, D)

    time_low = time_features(all_times).astype(LOW)
    hidden_time = matmul("nf,fd->nd", time_low, time_one)
    swish_time = jax.nn.silu(hidden_time).astype(LOW)
    condition_time = matmul("nf,fd->nd", swish_time, time_two)
    label_hot = (
        all_labels[:, None] == lax.broadcasted_iota(jnp.int32, (latent_count, CLASSES), 1)
    ).astype(LOW)
    class_own = matmul("nc,cd->nd", label_hot, class_table.astype(LOW))
    condition = lax.dynamic_slice_in_dim(condition_time, dp_rank * part, part, 1) + class_own
    condition_low = jax.nn.silu(condition).astype(LOW)
    modulation_low = modulation_weight.astype(LOW)
    partial = matmul("nd,dm->nm", condition_low, modulation_low)
    own_rows = scatter_own_order(partial.reshape(size, samples, -1), "dp")
    spread = gather_own_order(own_rows, "tensor")
    modulation = lax.dynamic_index_in_dim(spread, tensor_rank, 1, keepdims=False)
    mods = flip_blocks(modulation.reshape(-1, D), size, dp_rank)
    mods = jnp.pad(mods, ((0, 16 - mods.shape[0]), (0, 0)))

    latent_image = own_sample(latents, tensor_rank)
    noise_image = own_sample(noise_draw, tensor_rank)
    time_value = own_sample(time_values, tensor_rank)
    weight = own_sample(loss_weight, tensor_rank)
    patch_low = patchify((1.0 - time_value) * latent_image + time_value * noise_image).astype(LOW)
    target = patchify(noise_image - latent_image)
    absolute = relative_columns(D, size, dp_rank)
    feature_own = lax.dynamic_slice_in_dim(features, tensor_rank * TPL, TPL, 0)
    order_matrix = (lax.iota(jnp.int32, ZD)[:, None] == absolute[None, :]).astype(LOW)
    feature_own = matmul("tz,zy->ty", feature_own, order_matrix).astype(LOW)

    x = matmul("tp,pd->td", patch_low, edge[0]) + grid_table(absolute)
    saved = []
    encoded = x
    for layer in range(L):
        start = x
        middle, joined, mixed, attended = attn_forward(x, mods, 6 * layer, gathered["a", layer])
        x, inner, branch = ffn_forward(middle, mods, 6 * layer + 3, gathered["f", layer])
        saved.append((start, joined, mixed, attended, middle, inner, branch))
        if layer == 0:
            encoded = x

    tokens = latent_count * TPL
    place = dp_rank ^ (tensor_rank * (size // 4))
    grad_encoded, cosine_sum, keep_p, send_p, keep_q, send_q = projector(
        encoded,
        feature_own,
        place.reshape(1),
        -LAMBDA_ALIGN / tokens,
        gathered["p"],
        gathered["q"],
    )
    upstream, end_grads, head_grad, square_sum = head(
        x, mods, 6 * L, edge[1], target, weight.reshape(1), 2.0 / (tokens * PATCH)
    )
    loss_part = (
        weight * square_sum[0, 0] / (TPL * PATCH) / latent_count
        - LAMBDA_ALIGN * cosine_sum[0, 0] / tokens
    )

    reduced = {
        "p": reduce_gradient(keep_p, send_p, "B"),
        "q": reduce_gradient(keep_q, send_q, "A"),
    }
    mod_grads = [None] * L
    for layer in reversed(range(L)):
        start, joined, mixed, attended, middle, inner, branch = saved[layer]
        if layer == 0:
            upstream = upstream + grad_encoded
        upstream, ffn_mods, keep, send = ffn_backward(
            upstream, middle, mods, 6 * layer + 3, inner, branch, gathered["f", layer]
        )
        reduced["f", layer] = reduce_gradient(keep, send, "BC"[layer])
        upstream, attn_mods, keep, send = attn_backward(
            upstream, start, mods, 6 * layer, joined, mixed, attended, gathered["a", layer]
        )
        reduced["a", layer] = reduce_gradient(keep, send, "A")
        mod_grads[layer] = [attn_mods[:3], ffn_mods[:3]]

    embed_grad = matmul("tp,td->pd", patch_low, upstream.astype(LOW))
    edge_grad = jnp.stack([embed_grad, head_grad]).reshape(2, PATCH, size, part)
    edge_grad = total(scatter_relative(jnp.moveaxis(edge_grad, 2, 0), "dp"), "tensor")

    mod_rows = jnp.concatenate(mod_grads[0] + mod_grads[1] + [end_grads[:2]], axis=0)
    mod_flat = flip_blocks(mod_rows, size, dp_rank).astype(LOW).reshape(-1)
    mod_wide = modulation_weight.shape[1]
    mod_all = gather_own_order(mod_flat, "tensor")
    mod_own = lax.dynamic_slice_in_dim(mod_all, tensor_rank * mod_wide, mod_wide, 1)
    mod_own = gather_own_order(mod_own, "dp").reshape(latent_count, mod_wide)
    modulation_grad = matmul("nd,nm->dm", condition_low, mod_own)
    grad_condition = total(matmul("nm,dm->nd", mod_own, modulation_low), "tensor")
    grad_condition = jax.vjp(jax.nn.silu, condition)[1](grad_condition)[0].astype(LOW)
    table_grad = matmul("nc,nd->cd", label_hot, grad_condition)
    grad_all = gather_own_order(grad_condition, "dp")
    grad_all = jnp.moveaxis(grad_all, 0, 1).reshape(latent_count, D)
    swish_own = lax.dynamic_slice_in_dim(swish_time, dp_rank * part, part, 1)
    time_two_grad = matmul("nf,nd->fd", swish_own, grad_all)
    grad_hidden = jax.vjp(jax.nn.silu, hidden_time)[1](matmul("nd,fd->nf", grad_all, time_two))[0]
    freq_part = FREQ // size
    time_own = lax.dynamic_slice_in_dim(time_low, dp_rank * freq_part, freq_part, 1)
    time_one_grad = matmul("nf,nd->fd", time_own, grad_hidden.astype(LOW))

    attn = [reduced["a", layer] for layer in range(L)]
    feed = [reduced["f", layer] for layer in range(L)]
    gradients = (
        jnp.stack([jnp.moveaxis(g[:, :QKV].reshape(part, 3, OUTC), 1, 0) for g in attn]),
        jnp.stack([transposed(g[:, QKV:]) for g in attn]),
        jnp.stack([g[:, :FFC] for g in feed]),
        jnp.stack([transposed(g[:, FFC:]) for g in feed]),
        modulation_grad,
        time_one_grad,
        time_two_grad,
        table_grad,
        edge_grad,
        reduced["p"][:, :PC],
        reduced["q"],
        transposed(reduced["p"][:, PC:]),
    )
    layout = (
        ("dp", "tensor"),
        ("tensor", "dp"),
        ("dp", "tensor"),
        ("tensor", "dp"),
        ("dp", "tensor"),
        ("dp", ""),
        ("dp", ""),
        ("", "dp"),
        ("", "dp"),
        ("dp", "tensor"),
        ("dp", "tensor"),
        ("tensor", "dp"),
    )
    return adafactor(gradients, layout, loss_part)


def sum_over(axis, parts):
    joined = jnp.concatenate([p.reshape(-1) for p in parts])
    joined = total(joined, axis)
    outs, at = [], 0
    for p in parts:
        count = math.prod(p.shape)
        outs.append(joined[at : at + count].reshape(p.shape))
        at += count
    return outs


def spread_over(axis, parts):
    joined = gather_own_order(jnp.concatenate([p.reshape(-1) for p in parts]), axis)
    outs, at = [], 0
    for p in parts:
        count = math.prod(p.shape)
        piece = joined[:, at : at + count].reshape((-1,) + p.shape)
        piece = jnp.moveaxis(piece, 0, -2)
        outs.append(piece.reshape(p.shape[:-1] + (-1,)))
        at += count
    return outs


def adafactor(gradients, layout, loss_part):
    def axis_count(axis):
        return lax.axis_size(axis) if axis else 1

    vectors = {}
    buckets = {"dp": [], "tensor": []}
    for i, (g, (row_axis, column_axis)) in enumerate(zip(gradients, layout)):
        square = g * g
        vectors[i, "row"] = jnp.sum(square, axis=-1)
        vectors[i, "col"] = jnp.sum(square, axis=-2)
        for kind, over in (("row", column_axis), ("col", row_axis)):
            if over:
                buckets[over].append((i, kind))
    for axis in ("tensor", "dp"):
        keys = buckets[axis]
        for key, value in zip(keys, sum_over(axis, [vectors[k] for k in keys])):
            vectors[key] = value
    sums = []
    for i, (g, (row_axis, column_axis)) in enumerate(zip(gradients, layout)):
        if row_axis == "dp":
            sums.append(jnp.sum(vectors[i, "col"], axis=-1))
        else:
            sums.append(jnp.sum(vectors[i, "row"], axis=-1))
    shared = [k for k, axes in enumerate(layout) if "tensor" not in axes]
    split = [k for k, axes in enumerate(layout) if "tensor" in axes]
    for k, value in zip(split, sum_over("tensor", [sums[k] for k in split])):
        sums[k] = value
    updates, square_sums, entries = [], [], []
    for i, (g, (row_axis, column_axis)) in enumerate(zip(gradients, layout)):
        row_full = g.shape[-2] * axis_count(row_axis)
        column_full = g.shape[-1] * axis_count(column_axis)
        entries.append(row_full * column_full)
        vectors[i, "row"] = vectors[i, "row"] / column_full + EPS_FACTOR
        vectors[i, "col"] = vectors[i, "col"] / row_full + EPS_FACTOR
        mean = (sums[i] / entries[i] + EPS_FACTOR)[..., None]
        row = vectors[i, "row"] / mean
        update = g * lax.rsqrt(row[..., :, None] * vectors[i, "col"][..., None, :])
        updates.append(update)
        square_sums.append(jnp.sum(update * update, axis=(-2, -1)))
    first = jnp.where(lax.axis_index("tensor") == 0, 1.0, 0.0)
    for k in shared:
        square_sums[k] = square_sums[k] * first
    packed = [s.reshape(-1) for s in square_sums] + [loss_part.reshape(-1)]
    packed = sum_over("dp", sum_over("tensor", packed))
    changes = []
    for update, square_sum, count in zip(updates, packed, entries):
        root_mean = jnp.sqrt(square_sum / count).reshape(update.shape[:-2] + (1, 1))
        changes.append(-RATE * (update / jnp.maximum(1.0, root_mean / CLIP_RMS)))
    for axis in ("dp", "tensor"):
        keys = [(i, "row") for i, axes in enumerate(layout) if axes[0] == axis]
        keys += [(i, "col") for i, axes in enumerate(layout) if axes[1] == axis]
        for key, value in zip(keys, spread_over(axis, [vectors[k] for k in keys])):
            vectors[key] = value
    count = len(gradients)
    rows = jnp.concatenate([vectors[i, "row"].reshape(-1) for i in range(count)])
    columns = jnp.concatenate([vectors[i, "col"].reshape(-1) for i in range(count)])
    return (*changes, rows, columns, packed[-1].reshape(()))


def solution(mesh):
    return jax.shard_map(
        body,
        mesh=mesh,
        in_specs=(
            P("dp", None, None, None),
            P("dp", None, None, None),
            P("dp"),
            P(),
            P("dp"),
            P("dp"),
            P("dp", None),
            P(None, None, "dp", "tensor"),
            P(None, "tensor", "dp"),
            P(None, "dp", "tensor"),
            P(None, "tensor", "dp"),
            P("dp", "tensor"),
            P("dp", None),
            P("dp", None),
            P(None, "dp"),
            P(None, None, "dp"),
            P("dp", "tensor"),
            P("dp", "tensor"),
            P("tensor", "dp"),
        ),
        out_specs=(
            P(None, None, "dp", "tensor"),
            P(None, "tensor", "dp"),
            P(None, "dp", "tensor"),
            P(None, "tensor", "dp"),
            P("dp", "tensor"),
            P("dp", None),
            P("dp", None),
            P(None, "dp"),
            P(None, None, "dp"),
            P("dp", "tensor"),
            P("dp", "tensor"),
            P("tensor", "dp"),
            P(),
            P(),
            P(),
        ),
        check_vma=False,
    )
```
